32 devices in a mesh: depth: 8 (over z, x), tile: 4 (over y, core).
Axes of the slice: x: 2, y: 2, z: 4, core: 2. Of those that a mesh axis runs over, the one named last changes fastest.
Arguments:
- vorticity: bfloat16 [32, 256, 1024], P('depth', None, 'tile'), may hold values from -6 to 6
- tf_color: float32 [3, 16], replicated, may hold values from 0.05 to 1
- tf_extinction: float32 [16], replicated, may hold values from 0.001 to 10
Outputs:
- final_image: float32 [4, 256, 1024], P(None, 'depth', 'tile')
The draws below stay inside these ranges and needn't reach their ends.
All inputs are finite; a program needn't handle non-finite values.
Results may differ from the reference program's by a relative error of at most 0.002.
Values may be sent and summed in bfloat16 or wider, within the bound.
A program may use at most 64 MiB of HBM per device.

```python
import math
import jax
import jax.numpy as jnp
from jax import lax

NX = 256
KNOTS = 16
NZ = 32
NY = 1024


def shard_levels(key, dims, split, least, top_value):
    def one(dim, parts):
        heights = jax.random.uniform(jax.random.fold_in(jax.random.fold_in(key, 6), dim), (parts,), jnp.float32, least / len(split), top_value / len(split))
        return jnp.repeat(jnp.exp(heights), dims[dim] // parts).reshape((-1,) + (1,) * (len(dims) - dim - 1))

    loudness = one(*split[0])
    for cut in split[1:]:
        loudness = loudness * one(*cut)
    return loudness


def noise(own_key, shape, width, reach, pieces=(), held_as=jnp.bfloat16):
    entries = jax.random.normal(own_key, shape, jnp.float32) * width
    if len(pieces) > 0:
        entries = shard_levels(own_key, shape, pieces, -0.22, 0.18) * entries
    return jnp.clip(entries, min=-reach, max=reach).astype(held_as)


def setup_inputs(seed: int = 0) -> dict:
    keys = jax.random.split(jax.random.key(seed), 4)
    return {
        "vorticity": noise(keys[0], (NZ, NX, NY), 1.0, 6.0, ((0, 8), (2, 4))),
        "tf_color": jnp.clip(jax.random.uniform(keys[1], (3, KNOTS), jnp.float32, 0.05, 1.0), 0.05, 1.0),
        "tf_extinction": jnp.clip(jnp.exp(jax.random.uniform(keys[2], (KNOTS,), jnp.float32, math.log(0.001), math.log(10.0))), 0.001, 10.0),
    }


def shade_sample(slab_below, slab_here, slab_above, tf_color, tf_extinction, thickness):
    middle = slab_here.astype(jnp.float32)
    grad_z = 0.5 * (slab_above[1:-1, 1:-1].astype(jnp.float32) - slab_below[1:-1, 1:-1].astype(jnp.float32))
    grad_x = 0.5 * (middle[2:, 1:-1] - middle[:-2, 1:-1])
    grad_y = 0.5 * (middle[1:-1, 2:] - middle[1:-1, :-2])
    scalar = middle[1:-1, 1:-1]
    facing = 0.48 * grad_x + 0.6 * grad_y + 0.64 * grad_z
    lighting = 0.55 + 0.45 * facing / jnp.sqrt(grad_x * grad_x + grad_y * grad_y + grad_z * grad_z + 0.25)
    count_knots = tf_extinction.shape[0]
    position = jnp.clip((scalar + 4.0) * ((count_knots - 1) / 8.0), 0.0, count_knots - 1.0)
    knot_points = jnp.arange(count_knots, dtype=jnp.float32)
    weights = jnp.maximum(0.0, 1.0 - jnp.abs(position[None] - knot_points[:, None, None]))
    colour_mix = jnp.einsum('ck,kxy->cxy', tf_color, weights, precision=lax.Precision.HIGHEST)
    extinction = jnp.einsum('k,kxy->xy', tf_extinction, weights, precision=lax.Precision.HIGHEST)
    opacity = 1.0 - jnp.exp(-extinction * thickness)
    return jnp.concatenate([opacity[None] * lighting[None] * colour_mix, opacity[None]], axis=0)

def reference(vorticity, tf_color, tf_extinction):
    padded = jnp.pad(vorticity, 1)
    total_slices = vorticity.shape[0]
    thickness = 1.0 / total_slices

    def advance(accumulated, slice_index):
        slab_below = lax.dynamic_index_in_dim(padded, slice_index, 0, keepdims=False)
        slab_here = lax.dynamic_index_in_dim(padded, slice_index + 1, 0, keepdims=False)
        slab_above = lax.dynamic_index_in_dim(padded, slice_index + 2, 0, keepdims=False)
        sample = shade_sample(slab_below, slab_here, slab_above, tf_color, tf_extinction, thickness)
        return (accumulated + (1.0 - accumulated[3:4]) * sample, None)
    blank_image = jnp.zeros((4, vorticity.shape[1], vorticity.shape[2]), jnp.float32)
    final_image = lax.scan(advance, blank_image, jnp.arange(total_slices, dtype=jnp.int32))[0]
    return final_image
```

```python
import functools

import jax
import jax.numpy as jnp
from jax import lax
from jax.experimental import pallas as pl
from jax.experimental.pallas import tpu as pltpu
from jax.sharding import PartitionSpec as P


def extended(cells, sides, width):
    for axis, dim in sides:
        count = lax.axis_size(axis)
        ends = count - 1
        head = lax.slice_in_dim(cells, 0, width, axis=dim)
        tail = lax.slice_in_dim(cells, cells.shape[dim] - width, cells.shape[dim], axis=dim)
        cells = jnp.concatenate(
            [
                lax.ppermute(tail, axis, [(i, (i + 1) % count) for i in range(ends)]),
                cells,
                lax.ppermute(head, axis, [((i + 1) % count, i) for i in range(ends)]),
            ],
            axis=dim,
        )
    return cells


def shade_sample(slab_below, slab_here, slab_above, tf_color, tf_extinction, thickness):
    middle = slab_here.astype(jnp.float32)
    grad_z = 0.5 * (
        slab_above[1:-1, 1:-1].astype(jnp.float32) - slab_below[1:-1, 1:-1].astype(jnp.float32)
    )
    grad_x = 0.5 * (middle[2:, 1:-1] - middle[:-2, 1:-1])
    grad_y = 0.5 * (middle[1:-1, 2:] - middle[1:-1, :-2])
    scalar = middle[1:-1, 1:-1]
    facing = 0.48 * grad_x + 0.6 * grad_y + 0.64 * grad_z
    lighting = 0.55 + 0.45 * facing / jnp.sqrt(
        grad_x * grad_x + grad_y * grad_y + grad_z * grad_z + 0.25
    )
    count_knots = tf_extinction.shape[0]
    position = jnp.clip((scalar + 4.0) * ((count_knots - 1) / 8.0), 0.0, count_knots - 1.0)
    knot_points = jnp.arange(count_knots, dtype=jnp.float32)
    weights = jnp.maximum(0.0, 1.0 - jnp.abs(position[None] - knot_points[:, None, None]))
    colour_mix = jnp.einsum("ck,kxy->cxy", tf_color, weights, precision=lax.Precision.HIGHEST)
    extinction = jnp.einsum("k,kxy->xy", tf_extinction, weights, precision=lax.Precision.HIGHEST)
    opacity = 1.0 - jnp.exp(-extinction * thickness)
    return jnp.concatenate([opacity[None] * lighting[None] * colour_mix, opacity[None]], axis=0)


def composite(nearer, farther):
    return nearer + (1.0 - nearer[3:4]) * farther


def local(vorticity, tf_color, tf_extinction):
    depth_count = lax.axis_size("depth")
    local_slices = vorticity.shape[0]
    tile_rows = vorticity.shape[1]
    tile_cols = vorticity.shape[2]
    thickness = 1.0 / (local_slices * depth_count)
    padded = extended(vorticity, (("depth", 0), ("tile", 2)), 1)
    widened = jnp.pad(padded, ((0, 0), (1, 1), (0, 0)))

    def march(slice_index, accumulated):
        slab_below = lax.dynamic_index_in_dim(widened, slice_index, 0, keepdims=False)
        slab_here = lax.dynamic_index_in_dim(widened, slice_index + 1, 0, keepdims=False)
        slab_above = lax.dynamic_index_in_dim(widened, slice_index + 2, 0, keepdims=False)
        sample = shade_sample(slab_below, slab_here, slab_above, tf_color, tf_extinction, thickness)
        return composite(accumulated, sample)

    blank_image = jnp.zeros((4, tile_rows, tile_cols), jnp.float32)
    partial_value = lax.fori_loop(0, local_slices, march, blank_image)
    block_rows = tile_rows // depth_count
    rounds = depth_count.bit_length() - 1
    stacked = partial_value.reshape(4, 1, tile_rows, tile_cols)
    pieces = lax.all_to_all(
        stacked.astype(jnp.bfloat16), "depth", split_axis=2, concat_axis=1, tiled=True
    ).astype(stacked.dtype)
    for halving in range(rounds):
        paired = pieces.reshape(4, pieces.shape[1] // 2, 2, block_rows, tile_cols)
        pieces = composite(paired[:, :, 0], paired[:, :, 1])
    final_image = pieces[:, 0]
    return final_image


MESH = pl.DeviceIdType.MESH
LANES = 128
SUBLANES = 8


def iota(shape, dim):
    return lax.broadcasted_iota(jnp.int32, shape, dim)


def stencil(chosen_up, chosen_down):
    return jnp.where(chosen_up, 0.5, jnp.where(chosen_down, -0.5, 0.0))


def render_kernel(
    depth_count,
    tile_count,
    vort_hbm,
    color_ref,
    extinction_ref,
    out_ref,
    brick,
    slabs,
    row_out,
    row_in,
    edge_out,
    edge_in,
    local_sem,
    own_sem,
    send_sem,
    recv_sem,
    row_send_sem,
    row_recv_sem,
    edge_send_sem,
    edge_recv_sem,
):
    local_slices, tile_rows, tile_cols = vort_hbm.shape
    rows = tile_rows // depth_count
    knots = extinction_ref.shape[0]
    thickness = 1.0 / (local_slices * depth_count)
    group = local_slices * rows
    depth = lax.axis_index("depth")
    tile = lax.axis_index("tile")
    left = lax.rem(tile + tile_count - 1, tile_count)
    right = lax.rem(tile + 1, tile_count)

    whole = pltpu.make_async_copy(vort_hbm, brick, local_sem)
    whole.start()

    def slot(block):
        return slabs.at[pl.ds(1 + block * local_slices, local_slices)]

    def block_rows(block):
        return vort_hbm.at[:, pl.ds(pl.multiple_of(block * rows, rows), rows), :]

    own = pltpu.make_async_copy(block_rows(depth), slot(depth), own_sem)
    own.start()

    barrier = pltpu.get_barrier_semaphore()
    for step in range(depth_count):
        peer = lax.rem(depth + step, depth_count)
        if step > 0:
            pl.semaphore_signal(barrier, inc=1, device_id=(peer, tile), device_id_type=MESH)
        for side in (left, right):
            pl.semaphore_signal(barrier, inc=1, device_id=(peer, side), device_id_type=MESH)
    pl.semaphore_wait(barrier, 3 * depth_count - 1)

    sends = []
    for step in range(1, depth_count):
        peer = lax.rem(depth + step, depth_count)
        copy = pltpu.make_async_remote_copy(
            src_ref=block_rows(peer),
            dst_ref=slot(depth),
            send_sem=send_sem.at[step],
            recv_sem=recv_sem.at[depth],
            device_id=(peer, tile),
            device_id_type=MESH,
        )
        copy.start()
        sends.append(copy)

    whole.wait()
    packed = depth_count * 2 * local_slices
    line = iota((packed, 1), 0)
    line_block = line // (2 * local_slices)
    line_slice = (line % (2 * local_slices)) // 2
    line_row = line_block * rows + jnp.where(line % 2 == 0, -1, rows)
    inside = (line_row >= 0) & (line_row < tile_rows)
    wanted = jnp.where(inside, line_slice * tile_rows + line_row, -1)
    pick = jnp.where(iota((packed, local_slices * tile_rows), 1) == wanted, 1.0, 0.0)
    flat = brick[...].reshape(local_slices * tile_rows, tile_cols)
    outside = jnp.dot(pick.astype(jnp.bfloat16), flat, preferred_element_type=jnp.float32)
    for block in range(depth_count):
        first = block * 2 * local_slices
        row_out[block] = outside[first : first + 2 * local_slices].astype(jnp.bfloat16)
    column = iota((SUBLANES, tile_cols), 1)
    ends = iota((SUBLANES, tile_cols), 0)
    pick_ends = ((ends == 0) & (column == 0)) | ((ends == 1) & (column == tile_cols - 1))
    by_block = jnp.concatenate(
        [
            brick[z, block * rows : (block + 1) * rows, :]
            for block in range(depth_count)
            for z in range(local_slices)
        ],
        axis=0,
    )
    columns = lax.dot_general(
        jnp.where(pick_ends, 1.0, 0.0).astype(jnp.bfloat16),
        by_block,
        (((1,), (1,)), ((), ())),
        preferred_element_type=jnp.float32,
    )
    for block in range(depth_count):
        for end in range(2):
            edge_out[end, block] = columns[end : end + 1, block * group : (block + 1) * group]

    row_in[depth] = row_out[depth]
    for step in range(depth_count):
        peer = lax.rem(depth + step, depth_count)
        if step > 0:
            copy = pltpu.make_async_remote_copy(
                src_ref=row_out.at[peer],
                dst_ref=row_in.at[depth],
                send_sem=row_send_sem.at[step],
                recv_sem=row_recv_sem.at[depth],
                device_id=(peer, tile),
                device_id_type=MESH,
            )
            copy.start()
            sends.append(copy)
        for end, beside in enumerate((left, right)):
            copy = pltpu.make_async_remote_copy(
                src_ref=edge_out.at[end, peer],
                dst_ref=edge_in.at[1 - end, depth],
                send_sem=edge_send_sem.at[end, step],
                recv_sem=edge_recv_sem.at[1 - end, depth],
                device_id=(peer, beside),
                device_id_type=MESH,
            )
            copy.start()
            sends.append(copy)

    blank = jnp.zeros((1, rows, tile_cols), jnp.bfloat16)
    slabs[0:1] = blank
    slabs[1 + depth_count * local_slices : 2 + depth_count * local_slices] = blank

    spread = (2 + local_slices) * rows
    extra = 2 * SUBLANES
    cell = iota((group, spread + extra), 0)
    source = iota((group, spread + extra), 1)
    cell_row = cell % rows
    in_slabs = source < spread
    up = in_slabs & (source == cell + rows + 1) & (cell_row < rows - 1)
    down = in_slabs & (source == cell + rows - 1) & (cell_row > 0)
    packed_line = spread + 2 * (cell // rows)
    up = up | ((source == packed_line + 1) & (cell_row == rows - 1))
    down = down | ((source == packed_line) & (cell_row == 0))
    along_x = stencil(up, down).astype(jnp.bfloat16)
    along_z = stencil(in_slabs & (source == cell + 2 * rows), in_slabs & (source == cell)).astype(jnp.bfloat16)
    to_col = iota((tile_cols, tile_cols), 1)
    from_col = iota((tile_cols, tile_cols), 0)
    along_y = stencil(from_col == to_col + 1, from_col == to_col - 1).astype(jnp.bfloat16)
    has_left = jnp.where(tile > 0, -0.5, 0.0)
    has_right = jnp.where(tile < tile_count - 1, 0.5, 0.0)
    place = jnp.where(
        (ends == 0) & (column == 0),
        has_left,
        jnp.where((ends == 1) & (column == tile_cols - 1), has_right, 0.0),
    ).astype(jnp.bfloat16)

    lane = iota((rows, LANES), 1)

    def table(read):
        value = jnp.zeros((rows, LANES), jnp.float32)
        for k in range(knots):
            value = jnp.where(lane == k, read(k), value)
        slope = jnp.zeros((rows, LANES), jnp.float32)
        for k in range(knots - 1):
            slope = jnp.where(lane == k, read(k + 1) - read(k), slope)
        return value, slope

    tables = [table(lambda k, c=c: color_ref[c, k]) for c in range(3)]
    tables.append(table(lambda k: -thickness * extinction_ref[k]))

    def lookup(which, index, part):
        value, slope = tables[which]
        pieces = []
        for first in range(0, tile_cols, LANES):
            at = index[:, first : first + LANES]
            base = jnp.take_along_axis(value, at, axis=1, mode="promise_in_bounds")
            rise = jnp.take_along_axis(slope, at, axis=1, mode="promise_in_bounds")
            pieces.append(base + part[:, first : first + LANES] * rise)
        return jnp.concatenate(pieces, axis=1)

    own.wait()
    forward = depth < depth_count // 2

    def wait_recv(dst, sem):
        pltpu.make_async_remote_copy(
            src_ref=dst,
            dst_ref=dst,
            send_sem=send_sem.at[0],
            recv_sem=sem,
            device_id=(depth, tile),
            device_id_type=MESH,
        ).wait_recv()

    def wait_block(block):
        @pl.when(block != depth)
        def _():
            wait_recv(slot(block), recv_sem.at[block])

    def over(near, far):
        clear = 1.0 - near[3]
        return tuple(n + clear * f for n, f in zip(near, far))

    def order(step):
        return jnp.where(forward, step, depth_count - 1 - step)

    wait_block(order(0))

    def march(step, total):
        block = order(step)

        @pl.when(step < depth_count - 1)
        def _():
            wait_block(order(step + 1))

        @pl.when(block != depth)
        def _():
            wait_recv(row_in.at[block], row_recv_sem.at[block])

        wait_recv(edge_in.at[0, block], edge_recv_sem.at[0, block])
        wait_recv(edge_in.at[1, block], edge_recv_sem.at[1, block])

        around = slabs[pl.ds(block * local_slices, local_slices + 2)].reshape(spread, tile_cols)
        lines = row_in[block].astype(jnp.float32)
        lines = jnp.concatenate(
            [lines, jnp.zeros((extra - 2 * local_slices, tile_cols), jnp.float32)], axis=0
        ).astype(jnp.bfloat16)
        around = jnp.concatenate([around, lines], axis=0)
        grads_x = jnp.dot(along_x, around, preferred_element_type=jnp.float32)
        grads_z = jnp.dot(along_z, around, preferred_element_type=jnp.float32)
        cells = slabs[pl.ds(1 + block * local_slices, local_slices)].reshape(group, tile_cols)
        edge_row = iota((SUBLANES, group), 0)
        edges = jnp.where(
            edge_row == 0, edge_in[0, block], jnp.where(edge_row == 1, edge_in[1, block], 0.0)
        )
        grads_y = jnp.dot(cells, along_y, preferred_element_type=jnp.float32) + lax.dot_general(
            edges.astype(jnp.bfloat16),
            place,
            (((0,), (0,)), ((), ())),
            preferred_element_type=jnp.float32,
        )
        partial = None
        for z in range(local_slices):
            here = slice(z * rows, (z + 1) * rows)
            gx, gy, gz = grads_x[here], grads_y[here], grads_z[here]
            scalar = cells[here].astype(jnp.float32)
            facing = 0.48 * gx + 0.6 * gy + 0.64 * gz
            lighting = 0.55 + 0.45 * facing * lax.rsqrt(gx * gx + gy * gy + gz * gz + 0.25)
            position = jnp.clip((scalar + 4.0) * ((knots - 1) / 8.0), 0.0, knots - 1.0)
            index = position.astype(jnp.int32)
            part = position - index.astype(jnp.float32)
            opacity = 1.0 - jnp.exp(lookup(3, index, part))
            lit = opacity * lighting
            sample = tuple(lit * lookup(c, index, part) for c in range(3)) + (opacity,)
            partial = sample if partial is None else over(partial, sample)
        near = tuple(jnp.where(forward, t, p) for t, p in zip(total, partial))
        far = tuple(jnp.where(forward, p, t) for t, p in zip(total, partial))
        return over(near, far)

    nothing = tuple(jnp.zeros((rows, tile_cols), jnp.float32) for _ in range(4))
    total = lax.fori_loop(0, depth_count, march, nothing)
    for channel in range(4):
        out_ref[channel] = total[channel]
    for copy in sends:
        copy.wait_send()


def render(vorticity, tf_color, tf_extinction):
    depth_count = lax.axis_size("depth")
    tile_count = lax.axis_size("tile")
    local_slices, tile_rows, tile_cols = vorticity.shape
    rows = tile_rows // depth_count
    group = local_slices * rows
    dma = pltpu.SemaphoreType.DMA
    return pl.pallas_call(
        functools.partial(render_kernel, depth_count, tile_count),
        out_shape=jax.ShapeDtypeStruct((4, rows, tile_cols), jnp.float32),
        in_specs=[
            pl.BlockSpec(memory_space=pl.ANY),
            pl.BlockSpec(memory_space=pltpu.SMEM),
            pl.BlockSpec(memory_space=pltpu.SMEM),
        ],
        out_specs=pl.BlockSpec(memory_space=pltpu.VMEM),
        scratch_shapes=[
            pltpu.VMEM((local_slices, tile_rows, tile_cols), jnp.bfloat16),
            pltpu.VMEM((depth_count * local_slices + 2, rows, tile_cols), jnp.bfloat16),
            pltpu.VMEM((depth_count, 2 * local_slices, tile_cols), jnp.bfloat16),
            pltpu.VMEM((depth_count, 2 * local_slices, tile_cols), jnp.bfloat16),
            pltpu.VMEM((2, depth_count, 1, group), jnp.float32),
            pltpu.VMEM((2, depth_count, 1, group), jnp.float32),
            dma,
            dma,
            dma((depth_count,)),
            dma((depth_count,)),
            dma((depth_count,)),
            dma((depth_count,)),
            dma((2, depth_count)),
            dma((2, depth_count)),
        ],
        compiler_params=pltpu.CompilerParams(collective_id=0, has_side_effects=True),
        name="render",
    )(vorticity, tf_color, tf_extinction)


def fits(vorticity, knots):
    local_slices, tile_rows, tile_cols = vorticity.shape
    depth_count = lax.axis_size("depth")
    rows = tile_rows // depth_count
    return (
        tile_rows % depth_count == 0
        and rows % (2 * SUBLANES) == 0
        and tile_cols % LANES == 0
        and (local_slices * rows) % LANES == 0
        and 2 * local_slices == SUBLANES
        and knots <= LANES
        and depth_count <= 16
        and lax.axis_size("tile") > 1
    )


def choose(vorticity, tf_color, tf_extinction):
    if fits(vorticity, tf_extinction.shape[0]):
        return render(vorticity, tf_color, tf_extinction)
    return local(vorticity, tf_color, tf_extinction)


def solution(mesh):
    placed = (P("depth", None, "tile"), P(), P())
    return jax.shard_map(
        choose, mesh=mesh, in_specs=placed, out_specs=P(None, "depth", "tile"), check_vma=False
    )
```

```python
import functools

import jax
import jax.numpy as jnp
from jax import lax
from jax.experimental import pallas as pl
from jax.experimental.pallas import tpu as pltpu
from jax.sharding import PartitionSpec as P


def extended(cells, sides, width):
    for axis, dim in sides:
        count = lax.axis_size(axis)
        ends = count - 1
        head = lax.slice_in_dim(cells, 0, width, axis=dim)
        tail = lax.slice_in_dim(cells, cells.shape[dim] - width, cells.shape[dim], axis=dim)
        cells = jnp.concatenate(
            [
                lax.ppermute(tail, axis, [(i, (i + 1) % count) for i in range(ends)]),
                cells,
                lax.ppermute(head, axis, [((i + 1) % count, i) for i in range(ends)]),
            ],
            axis=dim,
        )
    return cells


def shade_sample(slab_below, slab_here, slab_above, tf_color, tf_extinction, thickness):
    middle = slab_here.astype(jnp.float32)
    grad_z = 0.5 * (
        slab_above[1:-1, 1:-1].astype(jnp.float32) - slab_below[1:-1, 1:-1].astype(jnp.float32)
    )
    grad_x = 0.5 * (middle[2:, 1:-1] - middle[:-2, 1:-1])
    grad_y = 0.5 * (middle[1:-1, 2:] - middle[1:-1, :-2])
    scalar = middle[1:-1, 1:-1]
    facing = 0.48 * grad_x + 0.6 * grad_y + 0.64 * grad_z
    lighting = 0.55 + 0.45 * facing / jnp.sqrt(
        grad_x * grad_x + grad_y * grad_y + grad_z * grad_z + 0.25
    )
    count_knots = tf_extinction.shape[0]
    position = jnp.clip((scalar + 4.0) * ((count_knots - 1) / 8.0), 0.0, count_knots - 1.0)
    knot_points = jnp.arange(count_knots, dtype=jnp.float32)
    weights = jnp.maximum(0.0, 1.0 - jnp.abs(position[None] - knot_points[:, None, None]))
    colour_mix = jnp.einsum("ck,kxy->cxy", tf_color, weights, precision=lax.Precision.HIGHEST)
    extinction = jnp.einsum("k,kxy->xy", tf_extinction, weights, precision=lax.Precision.HIGHEST)
    opacity = 1.0 - jnp.exp(-extinction * thickness)
    return jnp.concatenate([opacity[None] * lighting[None] * colour_mix, opacity[None]], axis=0)


def composite(nearer, farther):
    return nearer + (1.0 - nearer[3:4]) * farther


def local(vorticity, tf_color, tf_extinction):
    depth_count = lax.axis_size("depth")
    local_slices = vorticity.shape[0]
    tile_rows = vorticity.shape[1]
    tile_cols = vorticity.shape[2]
    thickness = 1.0 / (local_slices * depth_count)
    padded = extended(vorticity, (("depth", 0), ("tile", 2)), 1)
    widened = jnp.pad(padded, ((0, 0), (1, 1), (0, 0)))

    def march(slice_index, accumulated):
        slab_below = lax.dynamic_index_in_dim(widened, slice_index, 0, keepdims=False)
        slab_here = lax.dynamic_index_in_dim(widened, slice_index + 1, 0, keepdims=False)
        slab_above = lax.dynamic_index_in_dim(widened, slice_index + 2, 0, keepdims=False)
        sample = shade_sample(slab_below, slab_here, slab_above, tf_color, tf_extinction, thickness)
        return composite(accumulated, sample)

    blank_image = jnp.zeros((4, tile_rows, tile_cols), jnp.float32)
    partial_value = lax.fori_loop(0, local_slices, march, blank_image)
    block_rows = tile_rows // depth_count
    rounds = depth_count.bit_length() - 1
    stacked = partial_value.reshape(4, 1, tile_rows, tile_cols)
    pieces = lax.all_to_all(
        stacked.astype(jnp.bfloat16), "depth", split_axis=2, concat_axis=1, tiled=True
    ).astype(stacked.dtype)
    for halving in range(rounds):
        paired = pieces.reshape(4, pieces.shape[1] // 2, 2, block_rows, tile_cols)
        pieces = composite(paired[:, :, 0], paired[:, :, 1])
    final_image = pieces[:, 0]
    return final_image


MESH = pl.DeviceIdType.MESH
LANES = 128
PAIR = 2
SUBLANES = 8


def iota(shape, dim):
    return lax.broadcasted_iota(jnp.int32, shape, dim)


def stencil(chosen_up, chosen_down):
    return jnp.where(chosen_up, 0.5, jnp.where(chosen_down, -0.5, 0.0))


def render_kernel(
    depth_count,
    tile_count,
    vort_hbm,
    color_ref,
    extinction_ref,
    out_ref,
    brick,
    slabs,
    row_out,
    row_in,
    edge_out,
    edge_in,
    part_out,
    part_in,
    part_own,
    local_sem,
    own_sem,
    send_sem,
    recv_sem,
    row_send_sem,
    row_recv_sem,
    edge_send_sem,
    edge_recv_sem,
    halo_send_sem,
    halo_recv_sem,
    part_send_sem,
    part_recv_sem,
):
    local_slices, pairs, _, rows, tile_cols = vort_hbm.shape
    tile_rows = depth_count * rows
    knots = extinction_ref.shape[0]
    thickness = 1.0 / (local_slices * depth_count)
    group = local_slices * rows
    pair_slices = PAIR * local_slices
    depth = lax.axis_index("depth")
    tile = lax.axis_index("tile")
    pair = depth // PAIR
    member = depth % PAIR
    mate = 1 - member
    left = lax.rem(tile + tile_count - 1, tile_count)
    right = lax.rem(tile + 1, tile_count)

    whole = pltpu.make_async_copy(vort_hbm, brick, local_sem)
    whole.start()

    def slot(chunk, which):
        return slabs.at[chunk, pl.ds(1 + which * local_slices, local_slices)]

    own = [
        pltpu.make_async_copy(vort_hbm.at[:, chunk, member], slot(chunk, member), own_sem.at[chunk])
        for chunk in range(pairs)
    ]
    for copy in own:
        copy.start()

    barrier = pltpu.get_barrier_semaphore()
    for step in range(1, depth_count):
        peer = lax.rem(depth + step, depth_count)
        pl.semaphore_signal(barrier, inc=1, device_id=(peer, tile), device_id_type=MESH)
    for which in range(PAIR):
        for side in (left, right):
            pl.semaphore_signal(
                barrier, inc=1, device_id=(pair * PAIR + which, side), device_id_type=MESH
            )
    pl.semaphore_wait(barrier, depth_count - 1 + 2 * PAIR)

    def remote(src, dst, sent, received, target):
        return pltpu.make_async_remote_copy(
            src_ref=src,
            dst_ref=dst,
            send_sem=sent,
            recv_sem=received,
            device_id=target,
            device_id_type=MESH,
        )

    def order(step):
        return pair ^ (pairs - 1 - step)

    sends = []
    for step in range(pairs):
        chunk = order(step)
        copy = remote(
            vort_hbm.at[:, chunk, mate],
            slot(chunk, member),
            send_sem.at[step],
            recv_sem.at[chunk],
            (pair * PAIR + mate, tile),
        )
        copy.start()
        sends.append(copy)

    def halo(which, beyond):
        at = PAIR * local_slices + 1 if beyond < 0 else 0
        return remote(
            vort_hbm.at[0 if beyond < 0 else local_slices - 1, :, which],
            slabs.at[:, at],
            halo_send_sem.at[which],
            halo_recv_sem.at[0 if beyond > 0 else 1],
            ((pair + beyond) * PAIR + which, tile),
        )

    to_below = (member == 0) & (pair > 0)
    to_above = (member == PAIR - 1) & (pair < pairs - 1)

    @pl.when(to_below)
    def _():
        for which in range(PAIR):
            halo(which, -1).start()

    @pl.when(to_above)
    def _():
        for which in range(PAIR):
            halo(which, 1).start()

    blank = jnp.zeros((pairs, 1, rows, tile_cols), jnp.bfloat16)

    @pl.when(pair == 0)
    def _():
        slabs[:, 0:1] = blank

    @pl.when(pair == pairs - 1)
    def _():
        slabs[:, pair_slices + 1 : pair_slices + 2] = blank

    whole.wait()
    packed = depth_count * 2 * local_slices
    line = iota((packed, 1), 0)
    line_block = line // (2 * local_slices)
    line_slice = (line % (2 * local_slices)) // 2
    line_row = line_block * rows + jnp.where(line % 2 == 0, -1, rows)
    inside = (line_row >= 0) & (line_row < tile_rows)
    wanted = jnp.where(inside, line_slice * tile_rows + line_row, -1)
    pick = jnp.where(iota((packed, local_slices * tile_rows), 1) == wanted, 1.0, 0.0)
    flat = brick[...].reshape(local_slices * tile_rows, tile_cols)
    outside = jnp.dot(pick.astype(jnp.bfloat16), flat, preferred_element_type=jnp.float32)
    for block in range(depth_count):
        first = block * 2 * local_slices
        row_out[block % PAIR, block // PAIR] = outside[first : first + 2 * local_slices].astype(jnp.bfloat16)
    column = iota((SUBLANES, tile_cols), 1)
    ends = iota((SUBLANES, tile_cols), 0)
    pick_ends = ((ends == 0) & (column == 0)) | ((ends == 1) & (column == tile_cols - 1))
    by_block = jnp.concatenate(
        [
            brick[z, block // PAIR, block % PAIR]
            for block in range(depth_count)
            for z in range(local_slices)
        ],
        axis=0,
    )
    columns = lax.dot_general(
        jnp.where(pick_ends, 1.0, 0.0).astype(jnp.bfloat16),
        by_block,
        (((1,), (1,)), ((), ())),
        preferred_element_type=jnp.float32,
    )
    for block in range(depth_count):
        for end in range(2):
            edge_out[end, block % PAIR, block // PAIR] = columns[end : end + 1, block * group : (block + 1) * group]

    row_in[member] = row_out[member]
    copy = remote(
        row_out.at[mate],
        row_in.at[member],
        row_send_sem,
        row_recv_sem,
        (pair * PAIR + mate, tile),
    )
    copy.start()
    sends.append(copy)
    for which in range(PAIR):
        for end, beside in enumerate((left, right)):
            copy = remote(
                edge_out.at[end, which],
                edge_in.at[1 - end, member],
                edge_send_sem.at[end, which],
                edge_recv_sem.at[1 - end, member],
                (pair * PAIR + which, beside),
            )
            copy.start()
            sends.append(copy)

    spread = (2 + local_slices) * rows
    extra = 2 * SUBLANES
    cell = iota((group, spread + extra), 0)
    source = iota((group, spread + extra), 1)
    cell_row = cell % rows
    in_slabs = source < spread
    up = in_slabs & (source == cell + rows + 1) & (cell_row < rows - 1)
    down = in_slabs & (source == cell + rows - 1) & (cell_row > 0)
    packed_line = spread + 2 * (cell // rows)
    up = up | ((source == packed_line + 1) & (cell_row == rows - 1))
    down = down | ((source == packed_line) & (cell_row == 0))
    along_x = stencil(up, down).astype(jnp.bfloat16)
    along_z = stencil(in_slabs & (source == cell + 2 * rows), in_slabs & (source == cell)).astype(jnp.bfloat16)
    to_col = iota((tile_cols, tile_cols), 1)
    from_col = iota((tile_cols, tile_cols), 0)
    along_y = stencil(from_col == to_col + 1, from_col == to_col - 1).astype(jnp.bfloat16)
    has_left = jnp.where(tile > 0, -0.5, 0.0)
    has_right = jnp.where(tile < tile_count - 1, 0.5, 0.0)
    place = jnp.where(
        (ends == 0) & (column == 0),
        has_left,
        jnp.where((ends == 1) & (column == tile_cols - 1), has_right, 0.0),
    ).astype(jnp.bfloat16)

    lane = iota((rows, LANES), 1)

    def table(read):
        value = jnp.zeros((rows, LANES), jnp.float32)
        for k in range(knots):
            value = jnp.where(lane == k, read(k), value)
        slope = jnp.zeros((rows, LANES), jnp.float32)
        for k in range(knots - 1):
            slope = jnp.where(lane == k, read(k + 1) - read(k), slope)
        return value, slope

    tables = [table(lambda k, c=c: color_ref[c, k]) for c in range(3)]
    tables.append(table(lambda k: -thickness * extinction_ref[k]))

    def lookup(which, index, part):
        value, slope = tables[which]
        pieces = []
        for first in range(0, tile_cols, LANES):
            at = index[:, first : first + LANES]
            base = jnp.take_along_axis(value, at, axis=1, mode="promise_in_bounds")
            rise = jnp.take_along_axis(slope, at, axis=1, mode="promise_in_bounds")
            pieces.append(base + part[:, first : first + LANES] * rise)
        return jnp.concatenate(pieces, axis=1)

    def wait_recv(dst, sem):
        remote(dst, dst, row_send_sem, sem, (depth, tile)).wait_recv()

    for copy in own:
        copy.wait()

    @pl.when(pair > 0)
    def _():
        wait_recv(slabs.at[:, 0], halo_recv_sem.at[0])

    @pl.when(pair < pairs - 1)
    def _():
        wait_recv(slabs.at[:, pair_slices + 1], halo_recv_sem.at[1])

    wait_recv(row_in.at[mate], row_recv_sem)
    for end in range(2):
        for which in range(PAIR):
            wait_recv(edge_in.at[end, which], edge_recv_sem.at[end, which])

    def over(near, far):
        clear = 1.0 - near[3]
        return tuple(n + clear * f for n, f in zip(near, far))

    def shade(chunk, which, partial):
        around = slabs[chunk, which * local_slices : (which + 1) * local_slices + 2].reshape(spread, tile_cols)
        lines = row_in[which, chunk].astype(jnp.float32)
        lines = jnp.concatenate(
            [lines, jnp.zeros((extra - 2 * local_slices, tile_cols), jnp.float32)], axis=0
        ).astype(jnp.bfloat16)
        around = jnp.concatenate([around, lines], axis=0)
        grads_x = jnp.dot(along_x, around, preferred_element_type=jnp.float32)
        grads_z = jnp.dot(along_z, around, preferred_element_type=jnp.float32)
        cells = slabs[chunk, 1 + which * local_slices : 1 + (which + 1) * local_slices].reshape(group, tile_cols)
        edge_row = iota((SUBLANES, group), 0)
        edges = jnp.where(
            edge_row == 0, edge_in[0, which, chunk], jnp.where(edge_row == 1, edge_in[1, which, chunk], 0.0)
        )
        grads_y = jnp.dot(cells, along_y, preferred_element_type=jnp.float32) + lax.dot_general(
            edges.astype(jnp.bfloat16),
            place,
            (((0,), (0,)), ((), ())),
            preferred_element_type=jnp.float32,
        )
        for z in range(local_slices):
            here = slice(z * rows, (z + 1) * rows)
            gx, gy, gz = grads_x[here], grads_y[here], grads_z[here]
            scalar = cells[here].astype(jnp.float32)
            facing = 0.48 * gx + 0.6 * gy + 0.64 * gz
            lighting = 0.55 + 0.45 * facing * lax.rsqrt(gx * gx + gy * gy + gz * gz + 0.25)
            position = jnp.clip((scalar + 4.0) * ((knots - 1) / 8.0), 0.0, knots - 1.0)
            index = position.astype(jnp.int32)
            part = position - index.astype(jnp.float32)
            opacity = 1.0 - jnp.exp(lookup(3, index, part))
            lit = opacity * lighting
            sample = tuple(lit * lookup(c, index, part) for c in range(3)) + (opacity,)
            partial = sample if partial is None else over(partial, sample)
        return partial

    def send_part(step):
        chunk = order(step)
        return remote(
            part_out.at[chunk],
            part_in.at[pair],
            part_send_sem.at[chunk],
            part_recv_sem.at[pair],
            (chunk * PAIR + member, tile),
        )

    def march(step, carry):
        chunk = order(step)
        wait_recv(slot(chunk, mate), recv_sem.at[chunk])
        partial = None
        for which in range(PAIR):
            partial = shade(chunk, which, partial)
        for channel in range(4):
            part_own[channel] = partial[channel]
            part_out[chunk, channel] = partial[channel].astype(jnp.bfloat16)

        @pl.when(step < pairs - 1)
        def _():
            send_part(step).start()

        return carry

    lax.fori_loop(0, pairs, march, 0)
    part_in[pair] = part_out[pair]
    for step in range(pairs - 1):
        wait_recv(part_in.at[order(step)], part_recv_sem.at[order(step)])
    total = None
    for source in range(pairs):
        layer = tuple(
            jnp.where(pair == source, part_own[c], part_in[source, c].astype(jnp.float32))
            for c in range(4)
        )
        total = layer if total is None else over(total, layer)
    for channel in range(4):
        out_ref[channel] = total[channel]
    for copy in sends:
        copy.wait_send()
    for step in range(pairs - 1):
        send_part(step).wait_send()

    @pl.when(to_below)
    def _():
        for which in range(PAIR):
            halo(which, -1).wait_send()

    @pl.when(to_above)
    def _():
        for which in range(PAIR):
            halo(which, 1).wait_send()


def render(vorticity, tf_color, tf_extinction):
    depth_count = lax.axis_size("depth")
    tile_count = lax.axis_size("tile")
    local_slices, tile_rows, tile_cols = vorticity.shape
    rows = tile_rows // depth_count
    group = local_slices * rows
    pairs = depth_count // PAIR
    dma = pltpu.SemaphoreType.DMA
    return pl.pallas_call(
        functools.partial(render_kernel, depth_count, tile_count),
        out_shape=jax.ShapeDtypeStruct((4, rows, tile_cols), jnp.float32),
        in_specs=[
            pl.BlockSpec(memory_space=pl.ANY),
            pl.BlockSpec(memory_space=pltpu.SMEM),
            pl.BlockSpec(memory_space=pltpu.SMEM),
        ],
        out_specs=pl.BlockSpec(memory_space=pltpu.VMEM),
        scratch_shapes=[
            pltpu.VMEM((local_slices, pairs, PAIR, rows, tile_cols), jnp.bfloat16),
            pltpu.VMEM((pairs, PAIR * local_slices + 2, rows, tile_cols), jnp.bfloat16),
            pltpu.VMEM((PAIR, pairs, 2 * local_slices, tile_cols), jnp.bfloat16),
            pltpu.VMEM((PAIR, pairs, 2 * local_slices, tile_cols), jnp.bfloat16),
            pltpu.VMEM((2, PAIR, pairs, 1, group), jnp.float32),
            pltpu.VMEM((2, PAIR, pairs, 1, group), jnp.float32),
            pltpu.VMEM((pairs, 4, rows, tile_cols), jnp.bfloat16),
            pltpu.VMEM((pairs, 4, rows, tile_cols), jnp.bfloat16),
            pltpu.VMEM((4, rows, tile_cols), jnp.float32),
            dma,
            dma((pairs,)),
            dma((pairs,)),
            dma((pairs,)),
            dma,
            dma,
            dma((2, PAIR)),
            dma((2, PAIR)),
            dma((PAIR,)),
            dma((2,)),
            dma((pairs,)),
            dma((pairs,)),
        ],
        compiler_params=pltpu.CompilerParams(collective_id=0, has_side_effects=True),
        name="render",
    )(vorticity.reshape(local_slices, pairs, PAIR, rows, tile_cols), tf_color, tf_extinction)


def fits(vorticity, knots):
    local_slices, tile_rows, tile_cols = vorticity.shape
    depth_count = lax.axis_size("depth")
    rows = tile_rows // depth_count
    return (
        tile_rows % depth_count == 0
        and rows % (2 * SUBLANES) == 0
        and tile_cols % LANES == 0
        and (local_slices * rows) % LANES == 0
        and 2 * local_slices == SUBLANES
        and knots <= LANES
        and depth_count % PAIR == 0
        and depth_count & (depth_count - 1) == 0
        and depth_count <= 16
        and lax.axis_size("tile") > 1
    )


def choose(vorticity, tf_color, tf_extinction):
    if fits(vorticity, tf_extinction.shape[0]):
        return render(vorticity, tf_color, tf_extinction)
    return local(vorticity, tf_color, tf_extinction)


def solution(mesh):
    placed = (P("depth", None, "tile"), P(), P())
    return jax.shard_map(
        choose, mesh=mesh, in_specs=placed, out_specs=P(None, "depth", "tile"), check_vma=False
    )
```

```python
import functools

import jax
import jax.numpy as jnp
from jax import lax
from jax.experimental import pallas as pl
from jax.experimental.pallas import tpu as pltpu
from jax.sharding import PartitionSpec as P


def extended(cells, sides, width):
    for axis, dim in sides:
        count = lax.axis_size(axis)
        ends = count - 1
        head = lax.slice_in_dim(cells, 0, width, axis=dim)
        tail = lax.slice_in_dim(cells, cells.shape[dim] - width, cells.shape[dim], axis=dim)
        cells = jnp.concatenate(
            [
                lax.ppermute(tail, axis, [(i, (i + 1) % count) for i in range(ends)]),
                cells,
                lax.ppermute(head, axis, [((i + 1) % count, i) for i in range(ends)]),
            ],
            axis=dim,
        )
    return cells


def shade_sample(slab_below, slab_here, slab_above, tf_color, tf_extinction, thickness):
    middle = slab_here.astype(jnp.float32)
    grad_z = 0.5 * (
        slab_above[1:-1, 1:-1].astype(jnp.float32) - slab_below[1:-1, 1:-1].astype(jnp.float32)
    )
    grad_x = 0.5 * (middle[2:, 1:-1] - middle[:-2, 1:-1])
    grad_y = 0.5 * (middle[1:-1, 2:] - middle[1:-1, :-2])
    scalar = middle[1:-1, 1:-1]
    facing = 0.48 * grad_x + 0.6 * grad_y + 0.64 * grad_z
    lighting = 0.55 + 0.45 * facing / jnp.sqrt(
        grad_x * grad_x + grad_y * grad_y + grad_z * grad_z + 0.25
    )
    count_knots = tf_extinction.shape[0]
    position = jnp.clip((scalar + 4.0) * ((count_knots - 1) / 8.0), 0.0, count_knots - 1.0)
    knot_points = jnp.arange(count_knots, dtype=jnp.float32)
    weights = jnp.maximum(0.0, 1.0 - jnp.abs(position[None] - knot_points[:, None, None]))
    colour_mix = jnp.einsum("ck,kxy->cxy", tf_color, weights, precision=lax.Precision.HIGHEST)
    extinction = jnp.einsum("k,kxy->xy", tf_extinction, weights, precision=lax.Precision.HIGHEST)
    opacity = 1.0 - jnp.exp(-extinction * thickness)
    return jnp.concatenate([opacity[None] * lighting[None] * colour_mix, opacity[None]], axis=0)


def composite(nearer, farther):
    return nearer + (1.0 - nearer[3:4]) * farther


def local(vorticity, tf_color, tf_extinction):
    depth_count = lax.axis_size("depth")
    local_slices = vorticity.shape[0]
    tile_rows = vorticity.shape[1]
    tile_cols = vorticity.shape[2]
    thickness = 1.0 / (local_slices * depth_count)
    padded = extended(vorticity, (("depth", 0), ("tile", 2)), 1)
    widened = jnp.pad(padded, ((0, 0), (1, 1), (0, 0)))

    def march(slice_index, accumulated):
        slab_below = lax.dynamic_index_in_dim(widened, slice_index, 0, keepdims=False)
        slab_here = lax.dynamic_index_in_dim(widened, slice_index + 1, 0, keepdims=False)
        slab_above = lax.dynamic_index_in_dim(widened, slice_index + 2, 0, keepdims=False)
        sample = shade_sample(slab_below, slab_here, slab_above, tf_color, tf_extinction, thickness)
        return composite(accumulated, sample)

    blank_image = jnp.zeros((4, tile_rows, tile_cols), jnp.float32)
    partial_value = lax.fori_loop(0, local_slices, march, blank_image)
    block_rows = tile_rows // depth_count
    rounds = depth_count.bit_length() - 1
    stacked = partial_value.reshape(4, 1, tile_rows, tile_cols)
    pieces = lax.all_to_all(
        stacked.astype(jnp.bfloat16), "depth", split_axis=2, concat_axis=1, tiled=True
    ).astype(stacked.dtype)
    for halving in range(rounds):
        paired = pieces.reshape(4, pieces.shape[1] // 2, 2, block_rows, tile_cols)
        pieces = composite(paired[:, :, 0], paired[:, :, 1])
    final_image = pieces[:, 0]
    return final_image


MESH = pl.DeviceIdType.MESH
LANES = 128
PAIR = 2
SUBLANES = 8


def iota(shape, dim):
    return lax.broadcasted_iota(jnp.int32, shape, dim)


def stencil(chosen_up, chosen_down):
    return jnp.where(chosen_up, 0.5, jnp.where(chosen_down, -0.5, 0.0))


def render_kernel(
    depth_count,
    tile_count,
    vort_hbm,
    color_ref,
    extinction_ref,
    out_ref,
    brick,
    slabs,
    row_out,
    row_in,
    edge_out,
    edge_in,
    part_out,
    part_in,
    part_own,
    local_sem,
    own_sem,
    send_sem,
    recv_sem,
    row_send_sem,
    row_recv_sem,
    edge_send_sem,
    edge_recv_sem,
    halo_send_sem,
    halo_recv_sem,
    part_send_sem,
    part_recv_sem,
):
    local_slices, pairs, _, rows, tile_cols = vort_hbm.shape
    tile_rows = depth_count * rows
    knots = extinction_ref.shape[0]
    thickness = 1.0 / (local_slices * depth_count)
    group = local_slices * rows
    pair_slices = PAIR * local_slices
    depth = lax.axis_index("depth")
    tile = lax.axis_index("tile")
    pair = depth // PAIR
    member = depth % PAIR
    mate = 1 - member
    left = lax.rem(tile + tile_count - 1, tile_count)
    right = lax.rem(tile + 1, tile_count)

    whole = pltpu.make_async_copy(vort_hbm, brick, local_sem)
    whole.start()

    def slot(chunk, which):
        return slabs.at[chunk, pl.ds(1 + which * local_slices, local_slices)]

    own = [
        pltpu.make_async_copy(vort_hbm.at[:, chunk, member], slot(chunk, member), own_sem.at[chunk])
        for chunk in range(pairs)
    ]
    for copy in own:
        copy.start()

    barrier = pltpu.get_barrier_semaphore()
    for step in range(1, depth_count):
        peer = lax.rem(depth + step, depth_count)
        pl.semaphore_signal(barrier, inc=1, device_id=(peer, tile), device_id_type=MESH)
    for which in range(PAIR):
        for side in (left, right):
            pl.semaphore_signal(
                barrier, inc=1, device_id=(pair * PAIR + which, side), device_id_type=MESH
            )
    whole.wait()
    packed = depth_count * 2 * local_slices
    line = iota((packed, 1), 0)
    line_block = line // (2 * local_slices)
    line_slice = (line % (2 * local_slices)) // 2
    line_row = line_block * rows + jnp.where(line % 2 == 0, -1, rows)
    inside = (line_row >= 0) & (line_row < tile_rows)
    wanted = jnp.where(inside, line_slice * tile_rows + line_row, -1)
    pick = jnp.where(iota((packed, local_slices * tile_rows), 1) == wanted, 1.0, 0.0)
    flat = brick[...].reshape(local_slices * tile_rows, tile_cols)
    outside = jnp.dot(pick.astype(jnp.bfloat16), flat, preferred_element_type=jnp.float32)
    for block in range(depth_count):
        first = block * 2 * local_slices
        row_out[block % PAIR, block // PAIR] = outside[first : first + 2 * local_slices].astype(jnp.bfloat16)
    column = iota((SUBLANES, tile_cols), 1)
    ends = iota((SUBLANES, tile_cols), 0)
    pick_ends = ((ends == 0) & (column == 0)) | ((ends == 1) & (column == tile_cols - 1))
    by_block = jnp.concatenate(
        [
            brick[z, block // PAIR, block % PAIR]
            for block in range(depth_count)
            for z in range(local_slices)
        ],
        axis=0,
    )
    columns = lax.dot_general(
        jnp.where(pick_ends, 1.0, 0.0).astype(jnp.bfloat16),
        by_block,
        (((1,), (1,)), ((), ())),
        preferred_element_type=jnp.float32,
    )
    for block in range(depth_count):
        for end in range(2):
            edge_out[end, block % PAIR, block // PAIR] = columns[end : end + 1, block * group : (block + 1) * group]

    spread = (2 + local_slices) * rows
    extra = 2 * SUBLANES
    cell = iota((group, spread + extra), 0)
    source = iota((group, spread + extra), 1)
    cell_row = cell % rows
    in_slabs = source < spread
    up = in_slabs & (source == cell + rows + 1) & (cell_row < rows - 1)
    down = in_slabs & (source == cell + rows - 1) & (cell_row > 0)
    packed_line = spread + 2 * (cell // rows)
    up = up | ((source == packed_line + 1) & (cell_row == rows - 1))
    down = down | ((source == packed_line) & (cell_row == 0))
    along_x = stencil(up, down).astype(jnp.bfloat16)
    along_z = stencil(in_slabs & (source == cell + 2 * rows), in_slabs & (source == cell)).astype(jnp.bfloat16)
    to_col = iota((tile_cols, tile_cols), 1)
    from_col = iota((tile_cols, tile_cols), 0)
    along_y = stencil(from_col == to_col + 1, from_col == to_col - 1).astype(jnp.bfloat16)
    has_left = jnp.where(tile > 0, -0.5, 0.0)
    has_right = jnp.where(tile < tile_count - 1, 0.5, 0.0)
    place = jnp.where(
        (ends == 0) & (column == 0),
        has_left,
        jnp.where((ends == 1) & (column == tile_cols - 1), has_right, 0.0),
    ).astype(jnp.bfloat16)

    lane = iota((rows, LANES), 1)

    def table(read):
        value = jnp.zeros((rows, LANES), jnp.float32)
        for k in range(knots):
            value = jnp.where(lane == k, read(k), value)
        slope = jnp.zeros((rows, LANES), jnp.float32)
        for k in range(knots - 1):
            slope = jnp.where(lane == k, read(k + 1) - read(k), slope)
        return value, slope

    tables = [table(lambda k, c=c: color_ref[c, k]) for c in range(3)]
    tables.append(table(lambda k: -thickness * extinction_ref[k]))

    def lookup(which, index, part):
        value, slope = tables[which]
        pieces = []
        for first in range(0, tile_cols, LANES):
            at = index[:, first : first + LANES]
            base = jnp.take_along_axis(value, at, axis=1, mode="promise_in_bounds")
            rise = jnp.take_along_axis(slope, at, axis=1, mode="promise_in_bounds")
            pieces.append(base + part[:, first : first + LANES] * rise)
        return jnp.concatenate(pieces, axis=1)

    blank = jnp.zeros((pairs, 1, rows, tile_cols), jnp.bfloat16)

    @pl.when(pair == 0)
    def _():
        slabs[:, 0:1] = blank

    @pl.when(pair == pairs - 1)
    def _():
        slabs[:, pair_slices + 1 : pair_slices + 2] = blank

    pl.semaphore_wait(barrier, depth_count - 1 + 2 * PAIR)

    def remote(src, dst, sent, received, target):
        return pltpu.make_async_remote_copy(
            src_ref=src,
            dst_ref=dst,
            send_sem=sent,
            recv_sem=received,
            device_id=target,
            device_id_type=MESH,
        )

    def order(step):
        return pair ^ (pairs - 1 - step)

    sends = []
    row_in[member] = row_out[member]
    copy = remote(
        row_out.at[mate],
        row_in.at[member],
        row_send_sem,
        row_recv_sem,
        (pair * PAIR + mate, tile),
    )
    copy.start()
    sends.append(copy)
    for which in range(PAIR):
        for end, beside in enumerate((left, right)):
            copy = remote(
                edge_out.at[end, which],
                edge_in.at[1 - end, member],
                edge_send_sem.at[end, which],
                edge_recv_sem.at[1 - end, member],
                (pair * PAIR + which, beside),
            )
            copy.start()
            sends.append(copy)

    def halo(which, beyond):
        at = PAIR * local_slices + 1 if beyond < 0 else 0
        return remote(
            vort_hbm.at[0 if beyond < 0 else local_slices - 1, :, which],
            slabs.at[:, at],
            halo_send_sem.at[which],
            halo_recv_sem.at[0 if beyond > 0 else 1],
            ((pair + beyond) * PAIR + which, tile),
        )

    to_below = (member == 0) & (pair > 0)
    to_above = (member == PAIR - 1) & (pair < pairs - 1)

    @pl.when(to_below)
    def _():
        for which in range(PAIR):
            halo(which, -1).start()

    @pl.when(to_above)
    def _():
        for which in range(PAIR):
            halo(which, 1).start()

    for step in range(pairs):
        chunk = order(step)
        copy = remote(
            vort_hbm.at[:, chunk, mate],
            slot(chunk, member),
            send_sem.at[step],
            recv_sem.at[chunk],
            (pair * PAIR + mate, tile),
        )
        copy.start()
        sends.append(copy)

    def wait_recv(dst, sem):
        remote(dst, dst, row_send_sem, sem, (depth, tile)).wait_recv()

    for copy in own:
        copy.wait()

    @pl.when(pair > 0)
    def _():
        wait_recv(slabs.at[:, 0], halo_recv_sem.at[0])

    @pl.when(pair < pairs - 1)
    def _():
        wait_recv(slabs.at[:, pair_slices + 1], halo_recv_sem.at[1])

    wait_recv(row_in.at[mate], row_recv_sem)
    for end in range(2):
        for which in range(PAIR):
            wait_recv(edge_in.at[end, which], edge_recv_sem.at[end, which])

    def over(near, far):
        clear = 1.0 - near[3]
        return tuple(n + clear * f for n, f in zip(near, far))

    def shade(chunk, which, partial):
        around = slabs[chunk, which * local_slices : (which + 1) * local_slices + 2].reshape(spread, tile_cols)
        lines = row_in[which, chunk].astype(jnp.float32)
        lines = jnp.concatenate(
            [lines, jnp.zeros((extra - 2 * local_slices, tile_cols), jnp.float32)], axis=0
        ).astype(jnp.bfloat16)
        around = jnp.concatenate([around, lines], axis=0)
        grads_x = jnp.dot(along_x, around, preferred_element_type=jnp.float32)
        grads_z = jnp.dot(along_z, around, preferred_element_type=jnp.float32)
        cells = slabs[chunk, 1 + which * local_slices : 1 + (which + 1) * local_slices].reshape(group, tile_cols)
        edge_row = iota((SUBLANES, group), 0)
        edges = jnp.where(
            edge_row == 0, edge_in[0, which, chunk], jnp.where(edge_row == 1, edge_in[1, which, chunk], 0.0)
        )
        grads_y = jnp.dot(cells, along_y, preferred_element_type=jnp.float32) + lax.dot_general(
            edges.astype(jnp.bfloat16),
            place,
            (((0,), (0,)), ((), ())),
            preferred_element_type=jnp.float32,
        )
        for z in range(local_slices):
            here = slice(z * rows, (z + 1) * rows)
            gx, gy, gz = grads_x[here], grads_y[here], grads_z[here]
            scalar = cells[here].astype(jnp.float32)
            facing = 0.48 * gx + 0.6 * gy + 0.64 * gz
            lighting = 0.55 + 0.45 * facing * lax.rsqrt(gx * gx + gy * gy + gz * gz + 0.25)
            position = jnp.clip((scalar + 4.0) * ((knots - 1) / 8.0), 0.0, knots - 1.0)
            index = position.astype(jnp.int32)
            part = position - index.astype(jnp.float32)
            opacity = 1.0 - jnp.exp(lookup(3, index, part))
            lit = opacity * lighting
            sample = tuple(lit * lookup(c, index, part) for c in range(3)) + (opacity,)
            partial = sample if partial is None else over(partial, sample)
        return partial

    def send_part(step):
        chunk = order(step)
        return remote(
            part_out.at[chunk],
            part_in.at[pair],
            part_send_sem.at[chunk],
            part_recv_sem.at[pair],
            (chunk * PAIR + member, tile),
        )

    def march(step, carry):
        chunk = order(step)
        wait_recv(slot(chunk, mate), recv_sem.at[chunk])
        partial = None
        for which in range(PAIR):
            partial = shade(chunk, which, partial)
        for channel in range(4):
            part_own[channel] = partial[channel]
            part_out[chunk, channel] = partial[channel].astype(jnp.bfloat16)

        @pl.when(step < pairs - 1)
        def _():
            send_part(step).start()

        return carry

    lax.fori_loop(0, pairs, march, 0)
    part_in[pair] = part_out[pair]
    for step in range(pairs - 1):
        wait_recv(part_in.at[order(step)], part_recv_sem.at[order(step)])
    total = None
    for source in range(pairs):
        layer = tuple(
            jnp.where(pair == source, part_own[c], part_in[source, c].astype(jnp.float32))
            for c in range(4)
        )
        total = layer if total is None else over(total, layer)
    for channel in range(4):
        out_ref[channel] = total[channel]
    for copy in sends:
        copy.wait_send()
    for step in range(pairs - 1):
        send_part(step).wait_send()

    @pl.when(to_below)
    def _():
        for which in range(PAIR):
            halo(which, -1).wait_send()

    @pl.when(to_above)
    def _():
        for which in range(PAIR):
            halo(which, 1).wait_send()


def render(vorticity, tf_color, tf_extinction):
    depth_count = lax.axis_size("depth")
    tile_count = lax.axis_size("tile")
    local_slices, tile_rows, tile_cols = vorticity.shape
    rows = tile_rows // depth_count
    group = local_slices * rows
    pairs = depth_count // PAIR
    dma = pltpu.SemaphoreType.DMA
    return pl.pallas_call(
        functools.partial(render_kernel, depth_count, tile_count),
        out_shape=jax.ShapeDtypeStruct((4, rows, tile_cols), jnp.float32),
        in_specs=[
            pl.BlockSpec(memory_space=pl.ANY),
            pl.BlockSpec(memory_space=pltpu.SMEM),
            pl.BlockSpec(memory_space=pltpu.SMEM),
        ],
        out_specs=pl.BlockSpec(memory_space=pltpu.VMEM),
        scratch_shapes=[
            pltpu.VMEM((local_slices, pairs, PAIR, rows, tile_cols), jnp.bfloat16),
            pltpu.VMEM((pairs, PAIR * local_slices + 2, rows, tile_cols), jnp.bfloat16),
            pltpu.VMEM((PAIR, pairs, 2 * local_slices, tile_cols), jnp.bfloat16),
            pltpu.VMEM((PAIR, pairs, 2 * local_slices, tile_cols), jnp.bfloat16),
            pltpu.VMEM((2, PAIR, pairs, 1, group), jnp.float32),
            pltpu.VMEM((2, PAIR, pairs, 1, group), jnp.float32),
            pltpu.VMEM((pairs, 4, rows, tile_cols), jnp.bfloat16),
            pltpu.VMEM((pairs, 4, rows, tile_cols), jnp.bfloat16),
            pltpu.VMEM((4, rows, tile_cols), jnp.float32),
            dma,
            dma((pairs,)),
            dma((pairs,)),
            dma((pairs,)),
            dma,
            dma,
            dma((2, PAIR)),
            dma((2, PAIR)),
            dma((PAIR,)),
            dma((2,)),
            dma((pairs,)),
            dma((pairs,)),
        ],
        compiler_params=pltpu.CompilerParams(collective_id=0, has_side_effects=True),
        name="render",
    )(vorticity.reshape(local_slices, pairs, PAIR, rows, tile_cols), tf_color, tf_extinction)


def fits(vorticity, knots):
    local_slices, tile_rows, tile_cols = vorticity.shape
    depth_count = lax.axis_size("depth")
    rows = tile_rows // depth_count
    return (
        tile_rows % depth_count == 0
        and rows % (2 * SUBLANES) == 0
        and tile_cols % LANES == 0
        and (local_slices * rows) % LANES == 0
        and 2 * local_slices == SUBLANES
        and knots <= LANES
        and depth_count % PAIR == 0
        and depth_count & (depth_count - 1) == 0
        and depth_count <= 16
        and lax.axis_size("tile") > 1
    )


def choose(vorticity, tf_color, tf_extinction):
    if fits(vorticity, tf_extinction.shape[0]):
        return render(vorticity, tf_color, tf_extinction)
    return local(vorticity, tf_color, tf_extinction)


def solution(mesh):
    placed = (P("depth", None, "tile"), P(), P())
    return jax.shard_map(
        choose, mesh=mesh, in_specs=placed, out_specs=P(None, "depth", "tile"), check_vma=False
    )
```

```python
import functools

import jax
import jax.numpy as jnp
from jax import lax
from jax.experimental import pallas as pl
from jax.experimental.pallas import tpu as pltpu
from jax.sharding import PartitionSpec as P


def extended(cells, sides, width):
    for axis, dim in sides:
        count = lax.axis_size(axis)
        ends = count - 1
        head = lax.slice_in_dim(cells, 0, width, axis=dim)
        tail = lax.slice_in_dim(cells, cells.shape[dim] - width, cells.shape[dim], axis=dim)
        cells = jnp.concatenate(
            [
                lax.ppermute(tail, axis, [(i, (i + 1) % count) for i in range(ends)]),
                cells,
                lax.ppermute(head, axis, [((i + 1) % count, i) for i in range(ends)]),
            ],
            axis=dim,
        )
    return cells


def shade_sample(slab_below, slab_here, slab_above, tf_color, tf_extinction, thickness):
    middle = slab_here.astype(jnp.float32)
    grad_z = 0.5 * (
        slab_above[1:-1, 1:-1].astype(jnp.float32) - slab_below[1:-1, 1:-1].astype(jnp.float32)
    )
    grad_x = 0.5 * (middle[2:, 1:-1] - middle[:-2, 1:-1])
    grad_y = 0.5 * (middle[1:-1, 2:] - middle[1:-1, :-2])
    scalar = middle[1:-1, 1:-1]
    facing = 0.48 * grad_x + 0.6 * grad_y + 0.64 * grad_z
    lighting = 0.55 + 0.45 * facing / jnp.sqrt(
        grad_x * grad_x + grad_y * grad_y + grad_z * grad_z + 0.25
    )
    count_knots = tf_extinction.shape[0]
    position = jnp.clip((scalar + 4.0) * ((count_knots - 1) / 8.0), 0.0, count_knots - 1.0)
    knot_points = jnp.arange(count_knots, dtype=jnp.float32)
    weights = jnp.maximum(0.0, 1.0 - jnp.abs(position[None] - knot_points[:, None, None]))
    colour_mix = jnp.einsum("ck,kxy->cxy", tf_color, weights, precision=lax.Precision.HIGHEST)
    extinction = jnp.einsum("k,kxy->xy", tf_extinction, weights, precision=lax.Precision.HIGHEST)
    opacity = 1.0 - jnp.exp(-extinction * thickness)
    return jnp.concatenate([opacity[None] * lighting[None] * colour_mix, opacity[None]], axis=0)


def composite(nearer, farther):
    return nearer + (1.0 - nearer[3:4]) * farther


def local(vorticity, tf_color, tf_extinction):
    depth_count = lax.axis_size("depth")
    local_slices = vorticity.shape[0]
    tile_rows = vorticity.shape[1]
    tile_cols = vorticity.shape[2]
    thickness = 1.0 / (local_slices * depth_count)
    padded = extended(vorticity, (("depth", 0), ("tile", 2)), 1)
    widened = jnp.pad(padded, ((0, 0), (1, 1), (0, 0)))

    def march(slice_index, accumulated):
        slab_below = lax.dynamic_index_in_dim(widened, slice_index, 0, keepdims=False)
        slab_here = lax.dynamic_index_in_dim(widened, slice_index + 1, 0, keepdims=False)
        slab_above = lax.dynamic_index_in_dim(widened, slice_index + 2, 0, keepdims=False)
        sample = shade_sample(slab_below, slab_here, slab_above, tf_color, tf_extinction, thickness)
        return composite(accumulated, sample)

    blank_image = jnp.zeros((4, tile_rows, tile_cols), jnp.float32)
    partial_value = lax.fori_loop(0, local_slices, march, blank_image)
    block_rows = tile_rows // depth_count
    rounds = depth_count.bit_length() - 1
    stacked = partial_value.reshape(4, 1, tile_rows, tile_cols)
    pieces = lax.all_to_all(
        stacked.astype(jnp.bfloat16), "depth", split_axis=2, concat_axis=1, tiled=True
    ).astype(stacked.dtype)
    for halving in range(rounds):
        paired = pieces.reshape(4, pieces.shape[1] // 2, 2, block_rows, tile_cols)
        pieces = composite(paired[:, :, 0], paired[:, :, 1])
    final_image = pieces[:, 0]
    return final_image


MESH = pl.DeviceIdType.MESH
LANES = 128
PAIR = 2
SUBLANES = 8


def iota(shape, dim):
    return lax.broadcasted_iota(jnp.int32, shape, dim)


def stencil(chosen_up, chosen_down):
    return jnp.where(chosen_up, 0.5, jnp.where(chosen_down, -0.5, 0.0))


def render_kernel(
    depth_count,
    tile_count,
    vort_hbm,
    color_ref,
    extinction_ref,
    out_ref,
    brick,
    slabs,
    row_out,
    row_in,
    edge_out,
    edge_in,
    part_out,
    part_in,
    part_own,
    local_sem,
    own_sem,
    send_sem,
    recv_sem,
    row_send_sem,
    row_recv_sem,
    edge_send_sem,
    edge_recv_sem,
    halo_send_sem,
    halo_recv_sem,
    part_send_sem,
    part_recv_sem,
):
    local_slices, pairs, _, rows, tile_cols = vort_hbm.shape
    tile_rows = depth_count * rows
    knots = extinction_ref.shape[0]
    thickness = 1.0 / (local_slices * depth_count)
    group = local_slices * rows
    pair_slices = PAIR * local_slices
    depth = lax.axis_index("depth")
    tile = lax.axis_index("tile")
    pair = depth // PAIR
    member = depth % PAIR
    mate = 1 - member
    left = lax.rem(tile + tile_count - 1, tile_count)
    right = lax.rem(tile + 1, tile_count)

    whole = pltpu.make_async_copy(vort_hbm, brick, local_sem)
    whole.start()

    def slot(chunk, which):
        return slabs.at[chunk, pl.ds(1 + which * local_slices, local_slices)]

    own = [
        pltpu.make_async_copy(vort_hbm.at[:, chunk, member], slot(chunk, member), own_sem.at[chunk])
        for chunk in range(pairs)
    ]
    for copy in own:
        copy.start()

    barrier = pltpu.get_barrier_semaphore()
    for step in range(depth_count - 1, 0, -1):
        peer = depth ^ step
        pl.semaphore_signal(barrier, inc=1, device_id=(peer, tile), device_id_type=MESH)
    for which in range(PAIR):
        for side in (left, right):
            pl.semaphore_signal(
                barrier, inc=1, device_id=(pair * PAIR + which, side), device_id_type=MESH
            )
    whole.wait()
    packed = depth_count * 2 * local_slices
    line = iota((packed, 1), 0)
    line_block = line // (2 * local_slices)
    line_slice = (line % (2 * local_slices)) // 2
    line_row = line_block * rows + jnp.where(line % 2 == 0, -1, rows)
    inside = (line_row >= 0) & (line_row < tile_rows)
    wanted = jnp.where(inside, line_slice * tile_rows + line_row, -1)
    pick = jnp.where(iota((packed, local_slices * tile_rows), 1) == wanted, 1.0, 0.0)
    flat = brick[...].reshape(local_slices * tile_rows, tile_cols)
    outside = jnp.dot(pick.astype(jnp.bfloat16), flat, preferred_element_type=jnp.float32)
    for block in range(depth_count):
        first = block * 2 * local_slices
        row_out[block % PAIR, block // PAIR] = outside[first : first + 2 * local_slices].astype(jnp.bfloat16)
    column = iota((SUBLANES, tile_cols), 1)
    ends = iota((SUBLANES, tile_cols), 0)
    pick_ends = ((ends == 0) & (column == 0)) | ((ends == 1) & (column == tile_cols - 1))
    by_block = jnp.concatenate(
        [
            brick[z, block // PAIR, block % PAIR]
            for block in range(depth_count)
            for z in range(local_slices)
        ],
        axis=0,
    )
    columns = lax.dot_general(
        jnp.where(pick_ends, 1.0, 0.0).astype(jnp.bfloat16),
        by_block,
        (((1,), (1,)), ((), ())),
        preferred_element_type=jnp.float32,
    )
    for block in range(depth_count):
        for end in range(2):
            edge_out[end, block % PAIR, block // PAIR] = columns[end : end + 1, block * group : (block + 1) * group]

    blank = jnp.zeros((pairs, 1, rows, tile_cols), jnp.bfloat16)

    @pl.when(pair == 0)
    def _():
        slabs[:, 0:1] = blank

    @pl.when(pair == pairs - 1)
    def _():
        slabs[:, pair_slices + 1 : pair_slices + 2] = blank

    pl.semaphore_wait(barrier, depth_count - 1 + 2 * PAIR)

    def remote(src, dst, sent, received, target):
        return pltpu.make_async_remote_copy(
            src_ref=src,
            dst_ref=dst,
            send_sem=sent,
            recv_sem=received,
            device_id=target,
            device_id_type=MESH,
        )

    def order(step):
        return pair ^ (pairs - 1 - step)

    sends = []
    row_in[member] = row_out[member]
    copy = remote(
        row_out.at[mate],
        row_in.at[member],
        row_send_sem,
        row_recv_sem,
        (pair * PAIR + mate, tile),
    )
    copy.start()
    sends.append(copy)
    for which in range(PAIR):
        for end, beside in enumerate((left, right)):
            copy = remote(
                edge_out.at[end, which],
                edge_in.at[1 - end, member],
                edge_send_sem.at[end, which],
                edge_recv_sem.at[1 - end, member],
                (pair * PAIR + which, beside),
            )
            copy.start()
            sends.append(copy)

    def halo(which, beyond):
        at = PAIR * local_slices + 1 if beyond < 0 else 0
        return remote(
            vort_hbm.at[0 if beyond < 0 else local_slices - 1, :, which],
            slabs.at[:, at],
            halo_send_sem.at[which],
            halo_recv_sem.at[0 if beyond > 0 else 1],
            ((pair + beyond) * PAIR + which, tile),
        )

    to_below = (member == 0) & (pair > 0)
    to_above = (member == PAIR - 1) & (pair < pairs - 1)

    @pl.when(to_below)
    def _():
        for which in range(PAIR):
            halo(which, -1).start()

    @pl.when(to_above)
    def _():
        for which in range(PAIR):
            halo(which, 1).start()

    for step in range(pairs):
        chunk = order(step)
        copy = remote(
            vort_hbm.at[:, chunk, mate],
            slot(chunk, member),
            send_sem.at[step],
            recv_sem.at[chunk],
            (pair * PAIR + mate, tile),
        )
        copy.start()
        sends.append(copy)

    spread = (2 + local_slices) * rows
    extra = 2 * SUBLANES
    cell = iota((group, spread + extra), 0)
    source = iota((group, spread + extra), 1)
    cell_row = cell % rows
    in_slabs = source < spread
    up = in_slabs & (source == cell + rows + 1) & (cell_row < rows - 1)
    down = in_slabs & (source == cell + rows - 1) & (cell_row > 0)
    packed_line = spread + 2 * (cell // rows)
    up = up | ((source == packed_line + 1) & (cell_row == rows - 1))
    down = down | ((source == packed_line) & (cell_row == 0))
    along_x = stencil(up, down).astype(jnp.bfloat16)
    along_z = stencil(in_slabs & (source == cell + 2 * rows), in_slabs & (source == cell)).astype(jnp.bfloat16)
    to_col = iota((tile_cols, tile_cols), 1)
    from_col = iota((tile_cols, tile_cols), 0)
    along_y = stencil(from_col == to_col + 1, from_col == to_col - 1).astype(jnp.bfloat16)
    has_left = jnp.where(tile > 0, -0.5, 0.0)
    has_right = jnp.where(tile < tile_count - 1, 0.5, 0.0)
    place = jnp.where(
        (ends == 0) & (column == 0),
        has_left,
        jnp.where((ends == 1) & (column == tile_cols - 1), has_right, 0.0),
    ).astype(jnp.bfloat16)

    lane = iota((rows, LANES), 1)

    def table(read):
        value = jnp.zeros((rows, LANES), jnp.float32)
        for k in range(knots):
            value = jnp.where(lane == k, read(k), value)
        slope = jnp.zeros((rows, LANES), jnp.float32)
        for k in range(knots - 1):
            slope = jnp.where(lane == k, read(k + 1) - read(k), slope)
        return value, slope

    tables = [table(lambda k, c=c: color_ref[c, k]) for c in range(3)]
    tables.append(table(lambda k: -thickness * extinction_ref[k]))

    def lookup(which, index, part):
        value, slope = tables[which]
        pieces = []
        for first in range(0, tile_cols, LANES):
            at = index[:, first : first + LANES]
            base = jnp.take_along_axis(value, at, axis=1, mode="promise_in_bounds")
            rise = jnp.take_along_axis(slope, at, axis=1, mode="promise_in_bounds")
            pieces.append(base + part[:, first : first + LANES] * rise)
        return jnp.concatenate(pieces, axis=1)

    def wait_recv(dst, sem):
        remote(dst, dst, row_send_sem, sem, (depth, tile)).wait_recv()

    for copy in own:
        copy.wait()

    @pl.when(pair > 0)
    def _():
        wait_recv(slabs.at[:, 0], halo_recv_sem.at[0])

    @pl.when(pair < pairs - 1)
    def _():
        wait_recv(slabs.at[:, pair_slices + 1], halo_recv_sem.at[1])

    wait_recv(row_in.at[mate], row_recv_sem)
    for end in range(2):
        for which in range(PAIR):
            wait_recv(edge_in.at[end, which], edge_recv_sem.at[end, which])

    def over(near, far):
        clear = 1.0 - near[3]
        return tuple(n + clear * f for n, f in zip(near, far))

    def shade(chunk, which, partial):
        around = slabs[chunk, which * local_slices : (which + 1) * local_slices + 2].reshape(spread, tile_cols)
        lines = row_in[which, chunk].astype(jnp.float32)
        lines = jnp.concatenate(
            [lines, jnp.zeros((extra - 2 * local_slices, tile_cols), jnp.float32)], axis=0
        ).astype(jnp.bfloat16)
        around = jnp.concatenate([around, lines], axis=0)
        grads_x = jnp.dot(along_x, around, preferred_element_type=jnp.float32)
        grads_z = jnp.dot(along_z, around, preferred_element_type=jnp.float32)
        cells = slabs[chunk, 1 + which * local_slices : 1 + (which + 1) * local_slices].reshape(group, tile_cols)
        edge_row = iota((SUBLANES, group), 0)
        edges = jnp.where(
            edge_row == 0, edge_in[0, which, chunk], jnp.where(edge_row == 1, edge_in[1, which, chunk], 0.0)
        )
        grads_y = jnp.dot(cells, along_y, preferred_element_type=jnp.float32) + lax.dot_general(
            edges.astype(jnp.bfloat16),
            place,
            (((0,), (0,)), ((), ())),
            preferred_element_type=jnp.float32,
        )
        for z in range(local_slices):
            here = slice(z * rows, (z + 1) * rows)
            gx, gy, gz = grads_x[here], grads_y[here], grads_z[here]
            scalar = cells[here].astype(jnp.float32)
            facing = 0.48 * gx + 0.6 * gy + 0.64 * gz
            lighting = 0.55 + 0.45 * facing * lax.rsqrt(gx * gx + gy * gy + gz * gz + 0.25)
            position = jnp.clip((scalar + 4.0) * ((knots - 1) / 8.0), 0.0, knots - 1.0)
            index = position.astype(jnp.int32)
            part = position - index.astype(jnp.float32)
            opacity = 1.0 - jnp.exp(lookup(3, index, part))
            lit = opacity * lighting
            sample = tuple(lit * lookup(c, index, part) for c in range(3)) + (opacity,)
            partial = sample if partial is None else over(partial, sample)
        return partial

    def send_part(step):
        chunk = order(step)
        return remote(
            part_out.at[chunk],
            part_in.at[pair],
            part_send_sem.at[chunk],
            part_recv_sem.at[pair],
            (chunk * PAIR + member, tile),
        )

    def march(step, carry):
        chunk = order(step)
        wait_recv(slot(chunk, mate), recv_sem.at[chunk])
        partial = None
        for which in range(PAIR):
            partial = shade(chunk, which, partial)
        for channel in range(4):
            part_own[channel] = partial[channel]
            part_out[chunk, channel] = partial[channel].astype(jnp.bfloat16)

        @pl.when(step < pairs - 1)
        def _():
            send_part(step).start()

        return carry

    lax.fori_loop(0, pairs, march, 0)
    part_in[pair] = part_out[pair]
    for step in range(pairs - 1):
        wait_recv(part_in.at[order(step)], part_recv_sem.at[order(step)])
    total = None
    for source in range(pairs):
        layer = tuple(
            jnp.where(pair == source, part_own[c], part_in[source, c].astype(jnp.float32))
            for c in range(4)
        )
        total = layer if total is None else over(total, layer)
    for channel in range(4):
        out_ref[channel] = total[channel]
    for copy in sends:
        copy.wait_send()
    for step in range(pairs - 1):
        send_part(step).wait_send()

    @pl.when(to_below)
    def _():
        for which in range(PAIR):
            halo(which, -1).wait_send()

    @pl.when(to_above)
    def _():
        for which in range(PAIR):
            halo(which, 1).wait_send()


def render(vorticity, tf_color, tf_extinction):
    depth_count = lax.axis_size("depth")
    tile_count = lax.axis_size("tile")
    local_slices, tile_rows, tile_cols = vorticity.shape
    rows = tile_rows // depth_count
    group = local_slices * rows
    pairs = depth_count // PAIR
    dma = pltpu.SemaphoreType.DMA
    return pl.pallas_call(
        functools.partial(render_kernel, depth_count, tile_count),
        out_shape=jax.ShapeDtypeStruct((4, rows, tile_cols), jnp.float32),
        in_specs=[
            pl.BlockSpec(memory_space=pl.ANY),
            pl.BlockSpec(memory_space=pltpu.SMEM),
            pl.BlockSpec(memory_space=pltpu.SMEM),
        ],
        out_specs=pl.BlockSpec(memory_space=pltpu.VMEM),
        scratch_shapes=[
            pltpu.VMEM((local_slices, pairs, PAIR, rows, tile_cols), jnp.bfloat16),
            pltpu.VMEM((pairs, PAIR * local_slices + 2, rows, tile_cols), jnp.bfloat16),
            pltpu.VMEM((PAIR, pairs, 2 * local_slices, tile_cols), jnp.bfloat16),
            pltpu.VMEM((PAIR, pairs, 2 * local_slices, tile_cols), jnp.bfloat16),
            pltpu.VMEM((2, PAIR, pairs, 1, group), jnp.float32),
            pltpu.VMEM((2, PAIR, pairs, 1, group), jnp.float32),
            pltpu.VMEM((pairs, 4, rows, tile_cols), jnp.bfloat16),
            pltpu.VMEM((pairs, 4, rows, tile_cols), jnp.bfloat16),
            pltpu.VMEM((4, rows, tile_cols), jnp.float32),
            dma,
            dma((pairs,)),
            dma((pairs,)),
            dma((pairs,)),
            dma,
            dma,
            dma((2, PAIR)),
            dma((2, PAIR)),
            dma((PAIR,)),
            dma((2,)),
            dma((pairs,)),
            dma((pairs,)),
        ],
        compiler_params=pltpu.CompilerParams(collective_id=0, has_side_effects=True),
        name="render",
    )(vorticity.reshape(local_slices, pairs, PAIR, rows, tile_cols), tf_color, tf_extinction)


def fits(vorticity, knots):
    local_slices, tile_rows, tile_cols = vorticity.shape
    depth_count = lax.axis_size("depth")
    rows = tile_rows // depth_count
    return (
        tile_rows % depth_count == 0
        and rows % (2 * SUBLANES) == 0
        and tile_cols % LANES == 0
        and (local_slices * rows) % LANES == 0
        and 2 * local_slices == SUBLANES
        and knots <= LANES
        and depth_count % PAIR == 0
        and depth_count & (depth_count - 1) == 0
        and depth_count <= 16
        and lax.axis_size("tile") > 1
    )


def choose(vorticity, tf_color, tf_extinction):
    if fits(vorticity, tf_extinction.shape[0]):
        return render(vorticity, tf_color, tf_extinction)
    return local(vorticity, tf_color, tf_extinction)


def solution(mesh):
    placed = (P("depth", None, "tile"), P(), P())
    return jax.shard_map(
        choose, mesh=mesh, in_specs=placed, out_specs=P(None, "depth", "tile"), check_vma=False
    )
```
